32 devices in a mesh: groups: 2 (over y), expert: 4 (over z), token: 4 (over x, core).
Axes of the slice: x: 2, y: 2, z: 4, core: 2. Of those that a mesh axis runs over, the one named last changes fastest.
Arguments:
- tokens: bfloat16 [512, 2048], P(('groups', 'expert'), 'token'), parts along dimension 0, may hold values from -6 to 6
- expert_ids: int32 [512, 8], P(('groups', 'expert')), parts along dimension 0, may hold values from 0 to 15, all different within a row; in each aligned block of 64 rows (0 to 63, 64 to 127, ...) at most 64 rows name the same one
- route_weights: float32 [512, 8], P(('groups', 'expert')), parts along dimension 0, may hold values from 0.1 to 0.4
- w_gate_up: bfloat16 [16, 2048, 1536], P('expert', 'token'), may hold values from -0.125 to 0.125
- w_down: bfloat16 [16, 768, 2048], P('expert', None, 'token'), may hold values from -0.21875 to 0.21875
Outputs:
- combined: bfloat16 [512, 2048], P(('groups', 'expert'), 'token'), parts along dimension 0
The draws below stay inside these ranges and needn't reach their ends.
There are 2 independent parts, one for each index of `groups`. The reference program is written for one: setup_inputs(seed, part) draws one part's arguments, and reference() takes and returns one part's arrays. A program takes and returns all parts, laid end to end along the dimension named above; an argument that names none is the same for every part. Nothing has to cross between parts.
Inputs may be any that keep to these rules, and one draw needn't show every extreme that they name: `expert_ids`: each row names 8 different experts. In each aligned block of 64 rows no expert is named by more than 64 rows, a bound that some block reaches.
All inputs are finite; a program needn't handle non-finite values.
Results may differ from the reference program's by a relative error of at most 0.02.
Values may be sent and summed in bfloat16 or wider, within the bound.
A program may use at most 64 MiB of HBM per device.

```python
import math
import jax
import jax.numpy as jnp
import numpy as np
from jax import lax

D = 2048
FF = 768
TOP = 8
TOK_DEV = 64
EXPERTS = 16
TOKENS = 256
CAP = 64
N_EXPERT = 4
N_TOKEN = 4


def levels(stream_key, shape, shards, least, largest):
    gain = 1.0
    for dim, parts in shards:
        heights = jax.random.uniform(jax.random.fold_in(jax.random.fold_in(stream_key, 6), dim), (parts,), jnp.float32, least / len(shards), largest / len(shards))
        gain = gain * jnp.repeat(jnp.exp(heights), shape[dim] // parts).reshape((-1,) + (1,) * (len(shape) - 1 - dim))
    return gain


def deal_out(rng, own, number, rows, number_of, top, reach, slope):
    sequence = jax.random.permutation(rng, number_of)
    packed, usual = shares(number_of, rows * top, reach, slope, True), shares(number_of, rows * top, reach, slope, False)
    places = jnp.arange(number_of)

    def named(sizes, offset_by):
        used = int((sizes > 0).sum())
        fixed = max(1, used // 4)
        passed = fixed + (places - fixed + offset_by * (used - fixed)) % max(1, number_of - fixed)
        return jnp.zeros((number_of,), jnp.int32).at[sequence[jnp.where(places < fixed, places, passed)]].set(jnp.asarray(sizes, jnp.int32))

    sizes = jnp.where(number % 4 == 0, named(packed, number // 4), named(usual, number - number // 4 - 1))
    mixed = jax.random.permutation(jax.random.fold_in(own, 3), number_of)
    source_of, sink = mixed[0:number_of // 2 * 2:2], mixed[1:number_of // 2 * 2:2]
    slack = jnp.minimum(sizes[source_of] - 1, reach - sizes[sink]) // 2
    slack = jnp.where((source_of == sequence[0]) | (sink == sequence[0]) | (sizes[sink] == 0), 0, jnp.maximum(slack, 0))
    passed = jax.random.randint(jax.random.fold_in(own, 4), (number_of // 2,), 0, 1 << 20) % (slack + 1)
    sizes = sizes.at[source_of].add(-passed).at[sink].add(passed)
    labels = jnp.searchsorted(jnp.cumsum(sizes), jnp.arange(rows * top), side="right").astype(jnp.int32)
    listing = labels.reshape(top, rows).T
    listing = listing[jax.random.permutation(jax.random.fold_in(own, 1), rows)]
    offset_by = jax.random.randint(jax.random.fold_in(own, 2), (rows, 1), 0, top)
    return jnp.take_along_axis(listing, (jnp.arange(top)[None, :] + offset_by) % top, axis=1)


def shares(count, total, most, slope, full):
    portions = [(1 << 20) // math.isqrt(rank ** slope) + 1 for rank in range(1, count + 1)]
    largest = most if full else min(most, max(-(-total // count), total * portions[0] // sum(portions)))
    least = 1 if total - largest >= count - 1 else 0
    counts, spare = [largest] + [least] * (count - 1), total - largest - least * (count - 1)
    while spare > 0:
        candidates = [i for i in range(1, count) if counts[i] < largest] or [i for i in range(1, count) if counts[i] < most]
        mass, budget = sum([portions[i] for i in candidates]), spare
        for i in candidates:
            more = min(most - counts[i], max(1, budget * portions[i] // mass), spare)
            counts[i] = counts[i] + more
            spare = spare - more
    return np.array(counts)


def centred(own_key, extent, scale, limit, split=(), kind=jnp.bfloat16):
    array = jax.random.normal(own_key, extent, jnp.float32) * scale
    if len(split) > 0:
        array = levels(own_key, extent, split, -0.22, 0.18) * array
    return jnp.clip(array, min=-limit, max=limit).astype(kind)


def setup_inputs(seed: int = 0, part: int = 0) -> dict:
    key_list = jax.random.split(jax.random.key(seed), 6)
    own_keys = jax.random.split(jax.random.fold_in(key_list[5], part), 6)
    tokens = centred(own_keys[0], (TOKENS, D), 1.0, 6.0, ((0, 4), (1, 4)))
    expert_ids_keys = jax.random.split(jax.random.fold_in(own_keys[1], 1), TOKENS // TOK_DEV)
    expert_ids_turns = jax.random.permutation(jax.random.fold_in(own_keys[1], 3), TOKENS // TOK_DEV)
    expert_ids = jax.vmap(lambda own, number: deal_out(jax.random.fold_in(own_keys[1], 2), own, number, TOK_DEV, EXPERTS, TOP, CAP, 2))(expert_ids_keys, expert_ids_turns).reshape((TOKENS, TOP))
    route_weights = jnp.clip(0.1 + 0.3 * jax.random.uniform(own_keys[2], (TOKENS, TOP), jnp.float32) ** levels(own_keys[2], (TOKENS, TOP), ((0, 4),), -0.2, 0.2), 0.1, 0.4)
    w_gate_up = centred(key_list[3], (EXPERTS, D, 2 * FF), D ** -0.5, 0.125, ((0, 4), (1, 4)))
    w_down = centred(key_list[4], (EXPERTS, FF, D), FF ** -0.5, 0.21875, ((0, 4), (2, 4)))
    return {"tokens": tokens, "expert_ids": expert_ids, "route_weights": route_weights, "w_gate_up": w_gate_up, "w_down": w_down}


def reference(tokens, expert_ids, route_weights, w_gate_up, w_down):
    slot_total = N_EXPERT * CAP
    flat_ids = expert_ids.reshape(-1)
    onehot = (flat_ids[:, None] == jnp.arange(EXPERTS, dtype=jnp.int32)[None, :]).astype(jnp.int32)
    rank_of = jnp.sum((jnp.cumsum(onehot, axis=0) - 1) * onehot, axis=1).astype(jnp.int32)
    position = (flat_ids * slot_total + rank_of).astype(jnp.int32)
    token_of = (jnp.arange(flat_ids.shape[0], dtype=jnp.int32) // TOP).astype(jnp.int32)
    slot_table = jnp.full((EXPERTS * slot_total,), TOKENS, jnp.int32).at[position].set(token_of)
    slot_table = slot_table.reshape(EXPERTS, slot_total)
    padded = jnp.concatenate([tokens, jnp.zeros((1, D), tokens.dtype)], axis=0)
    block_cols = D // N_TOKEN

    def one_expert(operand):
        rows_of, gate_up_w, down_w = operand
        row_block = jnp.take(padded, rows_of, axis=0)
        split_in = row_block.reshape(slot_total, N_TOKEN, block_cols).astype(jnp.float32)
        split_w = gate_up_w.reshape(N_TOKEN, block_cols, 2 * FF).astype(jnp.float32)
        partial_j = jnp.einsum("rjd,jdf->jrf", split_in, split_w).astype(jnp.bfloat16)
        gate_up = jnp.sum(partial_j.astype(jnp.float32), axis=0)
        hidden = (jax.nn.silu(gate_up[:, :FF]) * gate_up[:, FF:]).astype(jnp.bfloat16)
        return jnp.dot(hidden, down_w, preferred_element_type=jnp.float32).astype(jnp.bfloat16)

    outputs = lax.map(one_expert, (slot_table, w_gate_up, w_down))
    picked = jnp.take(outputs.reshape(EXPERTS * slot_total, D), position, axis=0).reshape(TOKENS, TOP, D)
    combined = jnp.sum(route_weights[:, :, None] * picked.astype(jnp.float32), axis=1)
    return combined.astype(jnp.bfloat16)
```

```python
import functools

import jax
import jax.numpy as jnp
from jax import lax
from jax.experimental import pallas as pl
from jax.experimental.pallas import tpu as pltpu
from jax.sharding import PartitionSpec as P

MESH = pl.DeviceIdType.MESH


def rank_slots(flat_ids, experts):
    onehot = (flat_ids[:, None] == jnp.arange(experts, dtype=jnp.int32)[None, :]).astype(jnp.int32)
    rank_of = jnp.sum((jnp.cumsum(onehot, axis=0) - 1) * onehot, axis=1)
    return (onehot, rank_of)


def gate_up_terms(inputs, w_gate_up):
    return jnp.einsum("erd,edf->ref", inputs, w_gate_up, preferred_element_type=jnp.float32)


def expert_block(inputs, gate_up_w, down_w):
    hidden_units = gate_up_w.shape[2] // 2
    summed = lax.psum_scatter(
        gate_up_terms(inputs, gate_up_w).astype(jnp.bfloat16),
        "token",
        scatter_dimension=0,
        tiled=True,
    ).astype(jnp.float32)
    hidden = (jax.nn.silu(summed[..., :hidden_units]) * summed[..., hidden_units:]).astype(
        jnp.bfloat16
    )
    produced = jnp.einsum(
        "reh,ehd->erd",
        lax.all_gather(hidden, "token", axis=0, tiled=True),
        down_w,
        preferred_element_type=jnp.float32,
    )
    return produced.astype(jnp.bfloat16)


def slot_device(tokens, expert_ids, route_weights, w_gate_up, w_down):
    tok_dev, feature_cols = tokens.shape
    top_k = expert_ids.shape[1]
    local_experts = w_gate_up.shape[0]
    n_expert = lax.axis_size("expert")
    experts = local_experts * n_expert
    capacity = max(2, min(tok_dev, tok_dev * top_k * 5 // (2 * experts)))
    slot_count = n_expert * capacity
    flat_ids = expert_ids.reshape(-1)
    onehot, rank_of = rank_slots(flat_ids, experts)
    position = (
        flat_ids % local_experts * slot_count + flat_ids // local_experts * capacity + rank_of
    )
    token_of = jnp.arange(flat_ids.shape[0], dtype=jnp.int32) // top_k
    slot_table = (
        jnp.full((local_experts * slot_count,), tok_dev, jnp.int32).at[position].set(token_of)
    )
    padded = jnp.concatenate([tokens, jnp.zeros((1, feature_cols), tokens.dtype)], axis=0)
    outgoing = jnp.take(padded, slot_table, axis=0).reshape(
        local_experts, n_expert, capacity, feature_cols
    )
    arrived = lax.all_to_all(outgoing, "expert", split_axis=1, concat_axis=1, tiled=True)
    inputs = arrived.reshape(local_experts, slot_count, feature_cols)
    expert_out = expert_block(inputs, w_gate_up, w_down)
    returned = lax.all_to_all(
        expert_out.reshape(local_experts, n_expert, capacity, feature_cols),
        "expert",
        split_axis=1,
        concat_axis=1,
        tiled=True,
    )
    picked = jnp.take(
        returned.reshape(local_experts * slot_count, feature_cols), position, axis=0
    ).reshape(tok_dev, top_k, feature_cols)
    combined = jnp.sum(route_weights[:, :, None] * picked.astype(jnp.float32), axis=1)
    return combined.astype(jnp.bfloat16)


def flip(index, bits):
    out, bit = index, 1
    while bit <= bits:
        if bits & bit:
            out = out + bit * (1 - 2 * ((index // bit) % 2))
        bit *= 2
    return out


def dense_kernel(
    order,
    tokens_ref,
    ids_ref,
    weights_ref,
    wg_hbm,
    wd_hbm,
    out_ref,
    wg,
    wd,
    tok,
    row_out,
    row_in,
    far_out,
    far_in,
    sum_out,
    sum_in,
    near_out,
    near_in,
    own,
    hid,
    back_out,
    back_in,
    total,
    wg_sem,
    wd_sem,
    tok_s,
    tok_r,
    row_s,
    row_r,
    far_s,
    far_r,
    sum_s,
    sum_r,
    near_s,
    near_r,
    hid_s,
    hid_r,
    back_s,
    back_r,
):
    z = lax.axis_index("expert")
    t = lax.axis_index("token")
    n_e = len(order)
    rows = tokens_ref.shape[0]
    half = own.shape[2] // 2
    local = wg.shape[0]
    f32, bf16 = jnp.float32, jnp.bfloat16
    mate, across = {"token": flip(t, 1)}, {"token": flip(t, 2)}

    barrier = pltpu.get_barrier_semaphore()
    partners = [{"expert": flip(z, k)} for k in order if k] + [mate, across]
    for partner in partners:
        pl.semaphore_signal(barrier, inc=1, device_id=partner, device_id_type=MESH)

    wg_copies, wd_copies = {}, {}
    for j in (3, 1, 2, 0):
        wg_copies[j] = pltpu.make_async_copy(wg_hbm.at[flip(t, j)], wg.at[j], wg_sem.at[j])
        wg_copies[j].start()
    for j in range(local):
        wd_copies[j] = pltpu.make_async_copy(wd_hbm.at[flip(t, j)], wd.at[j], wd_sem.at[j])
        wd_copies[j].start()

    lanes = row_out.shape[2]
    eye = lax.broadcasted_iota(jnp.int32, (rows, lanes), 0) == lax.broadcasted_iota(
        jnp.int32, (rows, lanes), 1
    )
    for k in order:
        expert = flip(z, k) * local + t
        column = jnp.sum(
            jnp.where(ids_ref[...] == expert, weights_ref[...], 0.0), axis=1, keepdims=True
        )
        row = jnp.sum(jnp.where(eye, column, 0.0), axis=0, keepdims=True)
        row_out[k] = jnp.broadcast_to(row, row_out.shape[1:])

    pl.semaphore_wait(barrier, len(partners))

    pending = []

    def send(src, dst, s_sem, r_sem, device):
        copy = pltpu.make_async_remote_copy(
            src_ref=src,
            dst_ref=dst,
            send_sem=s_sem,
            recv_sem=r_sem,
            device_id=device,
            device_id_type=MESH,
        )
        copy.start()
        pending.append(copy)
        return copy

    tok_c, row_c, far_c, sum_c, near_c, back_c = {}, {}, {}, {}, {}, {}
    hid_c = {}
    for k in order:
        if k:
            tok_c[k] = send(
                tokens_ref, tok.at[k], tok_s.at[k], tok_r.at[k], {"expert": flip(z, k)}
            )
    for k in order:
        if k:
            row_c[k] = send(
                row_out.at[k], row_in.at[k], row_s.at[k], row_r.at[k], {"expert": flip(z, k)}
            )

    def terms(k, j):
        x = tok[k] if k else tokens_ref[...]
        return jnp.dot(x, wg[j], preferred_element_type=f32)

    def stage_a(k):
        first = k == order[0]
        if k:
            tok_c[k].wait_recv()
        if first:
            wg_copies[3].wait()
        far_out[k] = terms(k, 3).astype(bf16)
        far_c[k] = send(far_out.at[k], far_in.at[k], far_s.at[k], far_r.at[k], mate)
        if first:
            wg_copies[1].wait()
        near_out[k] = terms(k, 1).astype(bf16)
        near_c[k] = send(near_out.at[k], near_in.at[k], near_s.at[k], near_r.at[k], mate)
        if first:
            wg_copies[2].wait()
        own[k] = terms(k, 2)
        far_c[k].wait_recv()
        sum_out[k] = (own[k] + far_in[k].astype(f32)).astype(bf16)
        sum_c[k] = send(sum_out.at[k], sum_in.at[k], sum_s.at[k], sum_r.at[k], across)
        if first:
            wg_copies[0].wait()
        own[k] = terms(k, 0)

    def stage_b(k):
        near_c[k].wait_recv()
        if k:
            row_c[k].wait_recv()
        row = row_in[k, :1, :] if k else row_out[k, :1, :]
        column = jnp.sum(jnp.where(eye, row, 0.0), axis=1, keepdims=True)
        sum_c[k].wait_recv()
        gate = own[k, :, :half] + near_in[k, :, :half].astype(f32) + sum_in[k, :, :half].astype(f32)
        up = own[k, :, half:] + near_in[k, :, half:].astype(f32) + sum_in[k, :, half:].astype(f32)
        hid[k, 0] = (gate / (1.0 + jnp.exp(-gate)) * up * column).astype(bf16)
        hid_c[k, 2] = send(hid.at[k, 0], hid.at[k, 2], hid_s.at[k, 2], hid_r.at[k, 2], across)
        hid_c[k, 1] = send(hid.at[k, 0], hid.at[k, 1], hid_s.at[k, 1], hid_r.at[k, 1], mate)

    def stage_f(k):
        hid_c[k, 2].wait_recv()
        hid_c[k, 3] = send(hid.at[k, 2], hid.at[k, 3], hid_s.at[k, 3], hid_r.at[k, 3], mate)

    def stage_c(k):
        if k == order[0]:
            for j in range(local):
                wd_copies[j].wait()
        acc = jnp.dot(hid[k, 0], wd[0], preferred_element_type=f32)
        hid_c[k, 1].wait_recv()
        acc = acc + jnp.dot(hid[k, 1], wd[1], preferred_element_type=f32)
        acc = acc + jnp.dot(hid[k, 2], wd[2], preferred_element_type=f32)
        hid_c[k, 3].wait_recv()
        acc = acc + jnp.dot(hid[k, 3], wd[3], preferred_element_type=f32)
        if k:
            back_out[k] = acc.astype(bf16)
            back_c[k] = send(
                back_out.at[k], back_in.at[k], back_s.at[k], back_r.at[k], {"expert": flip(z, k)}
            )
        else:
            total[...] = acc

    n = n_e
    for step in range(n + 3):
        if step < n:
            stage_a(order[step])
        if 0 <= step - 2 < n:
            stage_f(order[step - 2])
        if 0 <= step - 1 < n:
            stage_b(order[step - 1])
        if 0 <= step - 2 < n:
            stage_c(order[step - 2])

    result = total[...]
    for k in order:
        if k:
            back_c[k].wait_recv()
            result = result + back_in[k].astype(f32)
    out_ref[...] = result.astype(out_ref.dtype)
    for copy in pending:
        copy.wait_send()


def dense_device(tokens, expert_ids, route_weights, w_gate_up, w_down):
    rows, feature_cols = tokens.shape
    local, _, wide = w_gate_up.shape
    hidden_units, out_cols = w_down.shape[1:]
    n_e = lax.axis_size("expert")
    order = tuple(sorted(range(n_e), key=lambda k: (k != 0, k == 1, k)))
    f32, bf16 = jnp.float32, jnp.bfloat16
    vmem = pl.BlockSpec(memory_space=pltpu.VMEM)
    hbm = pl.BlockSpec(memory_space=pl.ANY)
    dma = pltpu.SemaphoreType.DMA
    lanes = -(-rows // 128) * 128
    return pl.pallas_call(
        functools.partial(dense_kernel, order),
        out_shape=jax.ShapeDtypeStruct((rows, out_cols), bf16),
        in_specs=[vmem, vmem, vmem, hbm, hbm],
        out_specs=vmem,
        scratch_shapes=[
            pltpu.VMEM(w_gate_up.shape, bf16),
            pltpu.VMEM(w_down.shape, bf16),
            pltpu.VMEM((n_e, rows, feature_cols), bf16),
            pltpu.VMEM((n_e, 8, lanes), f32),
            pltpu.VMEM((n_e, 8, lanes), f32),
            *[pltpu.VMEM((n_e, rows, wide), bf16)] * 6,
            pltpu.VMEM((n_e, rows, wide), f32),
            pltpu.VMEM((n_e, local, rows, hidden_units), bf16),
            pltpu.VMEM((n_e, rows, out_cols), bf16),
            pltpu.VMEM((n_e, rows, out_cols), bf16),
            pltpu.VMEM((rows, out_cols), f32),
            dma((local,)),
            dma((local,)),
            *[dma((n_e,))] * 10,
            dma((n_e, local)),
            dma((n_e, local)),
            dma((n_e,)),
            dma((n_e,)),
        ],
        compiler_params=pltpu.CompilerParams(
            collective_id=0, has_side_effects=True, vmem_limit_bytes=48 * 1024 * 1024
        ),
    )(tokens, expert_ids, route_weights, w_gate_up, w_down)


def per_device(tokens, expert_ids, route_weights, w_gate_up, w_down):
    tok_dev = tokens.shape[0]
    top_k = expert_ids.shape[1]
    local_experts = w_gate_up.shape[0]
    n_expert, n_token = lax.axis_size("expert"), lax.axis_size("token")
    experts = local_experts * n_expert
    capacity = max(2, min(tok_dev, tok_dev * top_k * 5 // (2 * experts)))
    dense = capacity >= tok_dev and n_expert & (n_expert - 1) == 0
    if dense and n_token == local_experts == 4:
        return dense_device(tokens, expert_ids, route_weights, w_gate_up, w_down)
    return slot_device(tokens, expert_ids, route_weights, w_gate_up, w_down)


def solution(mesh):
    return jax.shard_map(
        per_device,
        mesh=mesh,
        in_specs=(
            P(("groups", "expert"), "token"),
            P(("groups", "expert"), None),
            P(("groups", "expert"), None),
            P("expert", "token", None),
            P("expert", None, "token"),
        ),
        out_specs=P(("groups", "expert"), "token"),
        check_vma=False,
    )
```

```python
import functools

import jax
import jax.numpy as jnp
from jax import lax
from jax.experimental import pallas as pl
from jax.experimental.pallas import tpu as pltpu
from jax.sharding import PartitionSpec as P

MESH = pl.DeviceIdType.MESH


def rank_slots(flat_ids, experts):
    onehot = (flat_ids[:, None] == jnp.arange(experts, dtype=jnp.int32)[None, :]).astype(jnp.int32)
    rank_of = jnp.sum((jnp.cumsum(onehot, axis=0) - 1) * onehot, axis=1)
    return (onehot, rank_of)


def gate_up_terms(inputs, w_gate_up):
    return jnp.einsum("erd,edf->ref", inputs, w_gate_up, preferred_element_type=jnp.float32)


def expert_block(inputs, gate_up_w, down_w):
    hidden_units = gate_up_w.shape[2] // 2
    summed = lax.psum_scatter(
        gate_up_terms(inputs, gate_up_w).astype(jnp.bfloat16),
        "token",
        scatter_dimension=0,
        tiled=True,
    ).astype(jnp.float32)
    hidden = (jax.nn.silu(summed[..., :hidden_units]) * summed[..., hidden_units:]).astype(
        jnp.bfloat16
    )
    produced = jnp.einsum(
        "reh,ehd->erd",
        lax.all_gather(hidden, "token", axis=0, tiled=True),
        down_w,
        preferred_element_type=jnp.float32,
    )
    return produced.astype(jnp.bfloat16)


def slot_device(tokens, expert_ids, route_weights, w_gate_up, w_down):
    tok_dev, feature_cols = tokens.shape
    top_k = expert_ids.shape[1]
    local_experts = w_gate_up.shape[0]
    n_expert = lax.axis_size("expert")
    experts = local_experts * n_expert
    capacity = max(2, min(tok_dev, tok_dev * top_k * 5 // (2 * experts)))
    slot_count = n_expert * capacity
    flat_ids = expert_ids.reshape(-1)
    onehot, rank_of = rank_slots(flat_ids, experts)
    position = (
        flat_ids % local_experts * slot_count + flat_ids // local_experts * capacity + rank_of
    )
    token_of = jnp.arange(flat_ids.shape[0], dtype=jnp.int32) // top_k
    slot_table = (
        jnp.full((local_experts * slot_count,), tok_dev, jnp.int32).at[position].set(token_of)
    )
    padded = jnp.concatenate([tokens, jnp.zeros((1, feature_cols), tokens.dtype)], axis=0)
    outgoing = jnp.take(padded, slot_table, axis=0).reshape(
        local_experts, n_expert, capacity, feature_cols
    )
    arrived = lax.all_to_all(outgoing, "expert", split_axis=1, concat_axis=1, tiled=True)
    inputs = arrived.reshape(local_experts, slot_count, feature_cols)
    expert_out = expert_block(inputs, w_gate_up, w_down)
    returned = lax.all_to_all(
        expert_out.reshape(local_experts, n_expert, capacity, feature_cols),
        "expert",
        split_axis=1,
        concat_axis=1,
        tiled=True,
    )
    picked = jnp.take(
        returned.reshape(local_experts * slot_count, feature_cols), position, axis=0
    ).reshape(tok_dev, top_k, feature_cols)
    combined = jnp.sum(route_weights[:, :, None] * picked.astype(jnp.float32), axis=1)
    return combined.astype(jnp.bfloat16)


def flip(index, bits):
    out, bit = index, 1
    while bit <= bits:
        if bits & bit:
            out = out + bit * (1 - 2 * ((index // bit) % 2))
        bit *= 2
    return out


def dense_kernel(
    chunks,
    tokens_ref,
    ids_ref,
    weights_ref,
    wg_hbm,
    wd_hbm,
    out_ref,
    wg,
    wd,
    tok,
    row_out,
    row_in,
    far_out,
    far_in,
    sum_out,
    sum_in,
    near_out,
    near_in,
    part,
    own,
    hid,
    back_out,
    back_in,
    total,
    load_sem,
    wg_sem,
    wd_sem,
    tok_s,
    tok_r,
    row_s,
    row_r,
    far_s,
    far_r,
    sum_s,
    sum_r,
    near_s,
    near_r,
    hid_s,
    hid_r,
    back_s,
    back_r,
):
    z = lax.axis_index("expert")
    t = lax.axis_index("token")
    rows = tokens_ref.shape[0]
    half = own.shape[2] // 2
    local = wg.shape[0]
    f32, bf16 = jnp.float32, jnp.bfloat16
    mate, across = {"token": flip(t, 1)}, {"token": flip(t, 2)}
    others = []
    for k, _, _ in chunks:
        if k and k not in others:
            others.append(k)
    others.sort()

    barrier = pltpu.get_barrier_semaphore()
    partners = [mate, across] + [{"expert": flip(z, k)} for k in others]
    for partner in reversed(partners):
        pl.semaphore_signal(barrier, inc=1, device_id=partner, device_id_type=MESH)

    load = pltpu.make_async_copy(tokens_ref, tok.at[0], load_sem)
    load.start()
    wg_copies, wd_copies = {}, {}
    for j in (3, 2, 1, 0):
        wg_copies[j] = pltpu.make_async_copy(wg_hbm.at[flip(t, j)], wg.at[j], wg_sem.at[j])
        wg_copies[j].start()

    for k in [0] + others:
        expert = flip(z, k) * local + t
        row = jnp.sum(
            jnp.where(ids_ref[...] == expert, weights_ref[...], 0.0), axis=0, keepdims=True
        )
        row_out[k] = jnp.broadcast_to(row, row_out.shape[1:])

    pending = []

    def send(src, dst, s_sem, r_sem, device):
        copy = pltpu.make_async_remote_copy(
            src_ref=src,
            dst_ref=dst,
            send_sem=s_sem,
            recv_sem=r_sem,
            device_id=device,
            device_id_type=MESH,
        )
        copy.start()
        pending.append(copy)
        return copy

    tok_c, row_c, far_c, sum_c, near_c, back_c = {}, {}, {}, {}, {}, {}
    hid_c = {}

    def terms(c, j):
        k, start, size = chunks[c]
        return jnp.dot(tok[k, pl.ds(start, size), :], wg[j], preferred_element_type=f32)

    def piece(c):
        k, start, size = chunks[c]
        return (k, pl.ds(start, size))

    def stage_a(c):
        k = chunks[c][0]
        here = piece(c)
        if k:
            tok_c[k].wait_recv()
        if c == 0:
            load.wait()
            wg_copies[3].wait()
        far_out[here] = terms(c, 3).astype(bf16)
        if c == 0:
            pl.semaphore_wait(barrier, len(partners))
        far_c[c] = send(far_out.at[here], far_in.at[here], far_s.at[c], far_r.at[c], mate)
        if c == 0:
            for o in others:
                there = {"expert": flip(z, o)}
                tok_c[o] = send(tokens_ref, tok.at[o], tok_s.at[o], tok_r.at[o], there)
            for j in range(local):
                wd_copies[j] = pltpu.make_async_copy(
                    wd_hbm.at[flip(t, j)], wd.at[j], wd_sem.at[j]
                )
                wd_copies[j].start()
            wg_copies[2].wait()
        part[here] = terms(c, 2)
        if c == 0:
            far_c[c].wait_recv()
            sum_out[here] = (part[here] + far_in[here].astype(f32)).astype(bf16)
            sum_c[c] = send(sum_out.at[here], sum_in.at[here], sum_s.at[c], sum_r.at[c], across)
            for o in others:
                there = {"expert": flip(z, o)}
                row_c[o] = send(row_out.at[o], row_in.at[o], row_s.at[o], row_r.at[o], there)
            wg_copies[1].wait()
        near_out[here] = terms(c, 1).astype(bf16)
        near_c[c] = send(near_out.at[here], near_in.at[here], near_s.at[c], near_r.at[c], mate)
        if c == 0:
            wg_copies[0].wait()
            own[here] = terms(c, 0)
            return
        far_c[c].wait_recv()
        sum_out[here] = (part[here] + far_in[here].astype(f32)).astype(bf16)
        sum_c[c] = send(sum_out.at[here], sum_in.at[here], sum_s.at[c], sum_r.at[c], across)
        own[here] = terms(c, 0)

    def stage_b(c):
        k, start, size = chunks[c]
        here = piece(c)
        near_c[c].wait_recv()
        if k:
            row_c[k].wait_recv()
        row = row_in[k, :1, :] if k else row_out[k, :1, :]
        eye = start + lax.broadcasted_iota(
            jnp.int32, (size, rows), 0
        ) == lax.broadcasted_iota(jnp.int32, (size, rows), 1)
        column = jnp.sum(jnp.where(eye, row, 0.0), axis=1, keepdims=True)
        sum_c[c].wait_recv()
        gate_up = own[here] + near_in[here].astype(f32) + sum_in[here].astype(f32)
        gate, up = gate_up[:, :half], gate_up[:, half:]
        at = pl.ds(start, size)
        hid[k, 0, at] = (gate / (1.0 + jnp.exp(-gate)) * up * column).astype(bf16)
        for j, device in ((2, across), (1, mate)):
            hid_c[c, j] = send(
                hid.at[k, 0, at], hid.at[k, j, at], hid_s.at[c, j], hid_r.at[c, j], device
            )

    def stage_f(c):
        k, start, size = chunks[c]
        at = pl.ds(start, size)
        hid_c[c, 2].wait_recv()
        hid_c[c, 3] = send(
            hid.at[k, 2, at], hid.at[k, 3, at], hid_s.at[c, 3], hid_r.at[c, 3], mate
        )

    def stage_c(c):
        k, start, size = chunks[c]
        at = pl.ds(start, size)
        if c == 0:
            for j in range(local):
                wd_copies[j].wait()
        acc = jnp.dot(hid[k, 0, at], wd[0], preferred_element_type=f32)
        hid_c[c, 1].wait_recv()
        acc = acc + jnp.dot(hid[k, 1, at], wd[1], preferred_element_type=f32)
        acc = acc + jnp.dot(hid[k, 2, at], wd[2], preferred_element_type=f32)
        hid_c[c, 3].wait_recv()
        acc = acc + jnp.dot(hid[k, 3, at], wd[3], preferred_element_type=f32)
        if k:
            back_out[k] = acc.astype(bf16)
            back_c[k] = send(
                back_out.at[k], back_in.at[k], back_s.at[k], back_r.at[k], {"expert": flip(z, k)}
            )
        else:
            total[at] = acc

    n = len(chunks)
    lead = 2
    for step in range(n + lead + 1):
        if step < n:
            stage_a(step)
        if 0 <= step - lead < n:
            stage_b(step - lead)
        if 0 <= step - lead - 1 < n:
            stage_f(step - lead - 1)
            stage_c(step - lead - 1)

    result = total[...]
    for k in others:
        back_c[k].wait_recv()
        result = result + back_in[k].astype(f32)
    out_ref[...] = result.astype(out_ref.dtype)
    for copy in pending:
        copy.wait_send()


def dense_device(tokens, expert_ids, route_weights, w_gate_up, w_down):
    rows, feature_cols = tokens.shape
    local, _, wide = w_gate_up.shape
    hidden_units, out_cols = w_down.shape[1:]
    n_e = lax.axis_size("expert")
    first = rows // 32 * 16
    chunks = ((0, 0, first),) + tuple((k, 0, rows) for k in (*range(2, n_e), 1))
    chunks += ((0, first, rows - first),)
    parts = len(chunks)
    f32, bf16 = jnp.float32, jnp.bfloat16
    vmem = pl.BlockSpec(memory_space=pltpu.VMEM)
    hbm = pl.BlockSpec(memory_space=pl.ANY)
    dma = pltpu.SemaphoreType.DMA
    return pl.pallas_call(
        functools.partial(dense_kernel, chunks),
        out_shape=jax.ShapeDtypeStruct((rows, out_cols), bf16),
        in_specs=[hbm, vmem, vmem, hbm, hbm],
        out_specs=vmem,
        scratch_shapes=[
            pltpu.VMEM(w_gate_up.shape, bf16),
            pltpu.VMEM(w_down.shape, bf16),
            pltpu.VMEM((n_e, rows, feature_cols), bf16),
            pltpu.VMEM((n_e, 8, rows), f32),
            pltpu.VMEM((n_e, 8, rows), f32),
            *[pltpu.VMEM((n_e, rows, wide), bf16)] * 6,
            *[pltpu.VMEM((n_e, rows, wide), f32)] * 2,
            pltpu.VMEM((n_e, local, rows, hidden_units), bf16),
            pltpu.VMEM((n_e, rows, out_cols), bf16),
            pltpu.VMEM((n_e, rows, out_cols), bf16),
            pltpu.VMEM((rows, out_cols), f32),
            dma,
            *[dma((local,))] * 2,
            *[dma((n_e,))] * 4,
            *[dma((parts,))] * 6,
            *[dma((parts, local))] * 2,
            dma((n_e,)),
            dma((n_e,)),
        ],
        compiler_params=pltpu.CompilerParams(
            collective_id=0, has_side_effects=True, vmem_limit_bytes=60 * 1024 * 1024
        ),
    )(tokens, expert_ids.T, route_weights.T, w_gate_up, w_down)


def per_device(tokens, expert_ids, route_weights, w_gate_up, w_down):
    tok_dev = tokens.shape[0]
    top_k = expert_ids.shape[1]
    local_experts = w_gate_up.shape[0]
    n_expert, n_token = lax.axis_size("expert"), lax.axis_size("token")
    experts = local_experts * n_expert
    capacity = max(2, min(tok_dev, tok_dev * top_k * 5 // (2 * experts)))
    dense = capacity >= tok_dev >= 32 and n_expert >= 2 and n_expert & (n_expert - 1) == 0
    if dense and tok_dev % 16 == 0 and n_token == local_experts == 4:
        return dense_device(tokens, expert_ids, route_weights, w_gate_up, w_down)
    return slot_device(tokens, expert_ids, route_weights, w_gate_up, w_down)


def solution(mesh):
    return jax.shard_map(
        per_device,
        mesh=mesh,
        in_specs=(
            P(("groups", "expert"), "token"),
            P(("groups", "expert"), None),
            P(("groups", "expert"), None),
            P("expert", "token", None),
            P("expert", None, "token"),
        ),
        out_specs=P(("groups", "expert"), "token"),
        check_vma=False,
    )
```

```python
import functools

import jax
import jax.numpy as jnp
from jax import lax
from jax.experimental import pallas as pl
from jax.experimental.pallas import tpu as pltpu
from jax.sharding import PartitionSpec as P

MESH = pl.DeviceIdType.MESH


def rank_slots(flat_ids, experts):
    onehot = (flat_ids[:, None] == jnp.arange(experts, dtype=jnp.int32)[None, :]).astype(jnp.int32)
    rank_of = jnp.sum((jnp.cumsum(onehot, axis=0) - 1) * onehot, axis=1)
    return (onehot, rank_of)


def gate_up_terms(inputs, w_gate_up):
    return jnp.einsum("erd,edf->ref", inputs, w_gate_up, preferred_element_type=jnp.float32)


def expert_block(inputs, gate_up_w, down_w):
    hidden_units = gate_up_w.shape[2] // 2
    summed = lax.psum_scatter(
        gate_up_terms(inputs, gate_up_w).astype(jnp.bfloat16),
        "token",
        scatter_dimension=0,
        tiled=True,
    ).astype(jnp.float32)
    hidden = (jax.nn.silu(summed[..., :hidden_units]) * summed[..., hidden_units:]).astype(
        jnp.bfloat16
    )
    produced = jnp.einsum(
        "reh,ehd->erd",
        lax.all_gather(hidden, "token", axis=0, tiled=True),
        down_w,
        preferred_element_type=jnp.float32,
    )
    return produced.astype(jnp.bfloat16)


def slot_device(tokens, expert_ids, route_weights, w_gate_up, w_down):
    tok_dev, feature_cols = tokens.shape
    top_k = expert_ids.shape[1]
    local_experts = w_gate_up.shape[0]
    n_expert = lax.axis_size("expert")
    experts = local_experts * n_expert
    capacity = max(2, min(tok_dev, tok_dev * top_k * 5 // (2 * experts)))
    slot_count = n_expert * capacity
    flat_ids = expert_ids.reshape(-1)
    onehot, rank_of = rank_slots(flat_ids, experts)
    position = (
        flat_ids % local_experts * slot_count + flat_ids // local_experts * capacity + rank_of
    )
    token_of = jnp.arange(flat_ids.shape[0], dtype=jnp.int32) // top_k
    slot_table = (
        jnp.full((local_experts * slot_count,), tok_dev, jnp.int32).at[position].set(token_of)
    )
    padded = jnp.concatenate([tokens, jnp.zeros((1, feature_cols), tokens.dtype)], axis=0)
    outgoing = jnp.take(padded, slot_table, axis=0).reshape(
        local_experts, n_expert, capacity, feature_cols
    )
    arrived = lax.all_to_all(outgoing, "expert", split_axis=1, concat_axis=1, tiled=True)
    inputs = arrived.reshape(local_experts, slot_count, feature_cols)
    expert_out = expert_block(inputs, w_gate_up, w_down)
    returned = lax.all_to_all(
        expert_out.reshape(local_experts, n_expert, capacity, feature_cols),
        "expert",
        split_axis=1,
        concat_axis=1,
        tiled=True,
    )
    picked = jnp.take(
        returned.reshape(local_experts * slot_count, feature_cols), position, axis=0
    ).reshape(tok_dev, top_k, feature_cols)
    combined = jnp.sum(route_weights[:, :, None] * picked.astype(jnp.float32), axis=1)
    return combined.astype(jnp.bfloat16)


def flip(index, bits):
    out, bit = index, 1
    while bit <= bits:
        if bits & bit:
            out = out + bit * (1 - 2 * ((index // bit) % 2))
        bit *= 2
    return out


def dense_kernel(
    chunks,
    tokens_ref,
    ids_hbm,
    weights_hbm,
    wg_hbm,
    wd_hbm,
    out_ref,
    wg,
    wd,
    ids_ref,
    weights_ref,
    tok,
    row_out,
    row_in,
    far_out,
    far_in,
    sum_out,
    sum_in,
    near_out,
    near_in,
    part,
    own,
    hid,
    back_out,
    back_in,
    total,
    load_sem,
    wg_sem,
    wd_sem,
    tok_s,
    tok_r,
    row_s,
    row_r,
    far_s,
    far_r,
    sum_s,
    sum_r,
    near_s,
    near_r,
    hid_s,
    hid_r,
    back_s,
    back_r,
):
    z = lax.axis_index("expert")
    t = lax.axis_index("token")
    rows = tokens_ref.shape[0]
    half = own.shape[2] // 2
    local = wg.shape[0]
    f32, bf16 = jnp.float32, jnp.bfloat16
    mate, across = {"token": flip(t, 1)}, {"token": flip(t, 2)}
    others = []
    for k, _, _ in chunks:
        if k and k not in others:
            others.append(k)

    barrier = pltpu.get_barrier_semaphore()
    partners = [mate, across] + [{"expert": flip(z, k)} for k in others]
    for partner in reversed(partners):
        pl.semaphore_signal(barrier, inc=1, device_id=partner, device_id_type=MESH)

    loads = [
        pltpu.make_async_copy(tokens_ref, tok.at[0], load_sem.at[0]),
        pltpu.make_async_copy(ids_hbm, ids_ref, load_sem.at[1]),
        pltpu.make_async_copy(weights_hbm, weights_ref, load_sem.at[2]),
    ]
    wg_copies, wd_copies = {}, {}
    for j in (3, 2, 1, 0):
        wg_copies[j] = pltpu.make_async_copy(wg_hbm.at[flip(t, j)], wg.at[j], wg_sem.at[j])
    for load in loads:
        load.start()
    for j in (3, 2):
        wg_copies[j].start()
    for load in loads:
        load.wait()

    for k in [0] + others:
        expert = flip(z, k) * local + t
        row = jnp.sum(
            jnp.where(ids_ref[...] == expert, weights_ref[...], 0.0), axis=0, keepdims=True
        )
        row_out[k] = jnp.broadcast_to(row, row_out.shape[1:])

    pending = []

    def send(src, dst, s_sem, r_sem, device):
        copy = pltpu.make_async_remote_copy(
            src_ref=src,
            dst_ref=dst,
            send_sem=s_sem,
            recv_sem=r_sem,
            device_id=device,
            device_id_type=MESH,
        )
        copy.start()
        pending.append(copy)
        return copy

    tok_c, row_c, far_c, sum_c, near_c, back_c = {}, {}, {}, {}, {}, {}
    hid_c = {}

    def terms(c, j):
        k, start, size = chunks[c]
        return jnp.dot(tok[k, pl.ds(start, size), :], wg[j], preferred_element_type=f32)

    def piece(c):
        k, start, size = chunks[c]
        return (k, pl.ds(start, size))

    def stage_a(c):
        k = chunks[c][0]
        here = piece(c)
        if k and chunks[c][1] == 0:
            tok_c[k].wait_recv()
        if c == 0:
            pl.semaphore_wait(barrier, len(partners))
            for o in others:
                there = {"expert": flip(z, o)}
                tok_c[o] = send(tokens_ref, tok.at[o], tok_s.at[o], tok_r.at[o], there)
            for j in (1, 0):
                wg_copies[j].start()
            wg_copies[3].wait()
        far_out[here] = terms(c, 3).astype(bf16)
        far_c[c] = send(far_out.at[here], far_in.at[here], far_s.at[c], far_r.at[c], mate)
        if c == 0:
            for j in range(local):
                wd_copies[j] = pltpu.make_async_copy(
                    wd_hbm.at[flip(t, j)], wd.at[j], wd_sem.at[j]
                )
                wd_copies[j].start()
            wg_copies[2].wait()
        part[here] = terms(c, 2)
        if c == 0:
            far_c[c].wait_recv()
            sum_out[here] = (part[here] + far_in[here].astype(f32)).astype(bf16)
            sum_c[c] = send(sum_out.at[here], sum_in.at[here], sum_s.at[c], sum_r.at[c], across)
            for o in others:
                there = {"expert": flip(z, o)}
                row_c[o] = send(row_out.at[o], row_in.at[o], row_s.at[o], row_r.at[o], there)
            wg_copies[1].wait()
        near_out[here] = terms(c, 1).astype(bf16)
        near_c[c] = send(near_out.at[here], near_in.at[here], near_s.at[c], near_r.at[c], mate)
        if c == 0:
            wg_copies[0].wait()
            own[here] = terms(c, 0)
            return
        far_c[c].wait_recv()
        sum_out[here] = (part[here] + far_in[here].astype(f32)).astype(bf16)
        sum_c[c] = send(sum_out.at[here], sum_in.at[here], sum_s.at[c], sum_r.at[c], across)
        own[here] = terms(c, 0)

    def stage_b(c):
        k, start, size = chunks[c]
        here = piece(c)
        near_c[c].wait_recv()
        if k and start == 0:
            row_c[k].wait_recv()
        row = row_in[k, :1, :] if k else row_out[k, :1, :]
        eye = start + lax.broadcasted_iota(
            jnp.int32, (size, rows), 0
        ) == lax.broadcasted_iota(jnp.int32, (size, rows), 1)
        column = jnp.sum(jnp.where(eye, row, 0.0), axis=1, keepdims=True)
        sum_c[c].wait_recv()
        gate_up = own[here] + near_in[here].astype(f32) + sum_in[here].astype(f32)
        gate, up = gate_up[:, :half], gate_up[:, half:]
        at = pl.ds(start, size)
        hid[k, 0, at] = (gate / (1.0 + jnp.exp(-gate)) * up * column).astype(bf16)
        for j, device in ((2, across), (1, mate)):
            hid_c[c, j] = send(
                hid.at[k, 0, at], hid.at[k, j, at], hid_s.at[c, j], hid_r.at[c, j], device
            )

    def stage_f(c):
        k, start, size = chunks[c]
        at = pl.ds(start, size)
        hid_c[c, 2].wait_recv()
        hid_c[c, 3] = send(
            hid.at[k, 2, at], hid.at[k, 3, at], hid_s.at[c, 3], hid_r.at[c, 3], mate
        )

    def stage_c(c):
        k, start, size = chunks[c]
        at = pl.ds(start, size)
        if c == 0:
            for j in range(local):
                wd_copies[j].wait()
        acc = jnp.dot(hid[k, 0, at], wd[0], preferred_element_type=f32)
        hid_c[c, 1].wait_recv()
        acc = acc + jnp.dot(hid[k, 1, at], wd[1], preferred_element_type=f32)
        acc = acc + jnp.dot(hid[k, 2, at], wd[2], preferred_element_type=f32)
        hid_c[c, 3].wait_recv()
        acc = acc + jnp.dot(hid[k, 3, at], wd[3], preferred_element_type=f32)
        if k:
            there = {"expert": flip(z, k)}
            back_out[k, at] = acc.astype(bf16)
            back_c[c] = send(
                back_out.at[k, at], back_in.at[k, at], back_s.at[c], back_r.at[c], there
            )
        else:
            total[at] = acc

    n = len(chunks)
    for step in range(n):
        stage_a(step)
        if step >= 2:
            stage_b(step - 2)
        if step >= 3:
            stage_f(step - 3)
            stage_c(step - 3)
    for step in range(max(n - 2, 0), n):
        stage_b(step)
    for step in range(max(n - 3, 0), n):
        stage_f(step)
        stage_c(step)

    for copy in back_c.values():
        copy.wait_recv()
    result = total[...]
    for k in others:
        result = result + back_in[k].astype(f32)
    out_ref[...] = result.astype(out_ref.dtype)
    for copy in pending:
        copy.wait_send()


def dense_device(tokens, expert_ids, route_weights, w_gate_up, w_down):
    rows, feature_cols = tokens.shape
    local, _, wide = w_gate_up.shape
    hidden_units, out_cols = w_down.shape[1:]
    n_e = lax.axis_size("expert")
    first = rows // 32 * 16
    chunks = ((0, 0, rows), (1, 0, first)) + tuple((k, 0, rows) for k in range(n_e - 1, 1, -1))
    chunks += ((1, first, rows - first),)
    parts = len(chunks)
    f32, bf16 = jnp.float32, jnp.bfloat16
    vmem = pl.BlockSpec(memory_space=pltpu.VMEM)
    hbm = pl.BlockSpec(memory_space=pltpu.MemorySpace.HBM)
    dma = pltpu.SemaphoreType.DMA
    return pl.pallas_call(
        functools.partial(dense_kernel, chunks),
        out_shape=jax.ShapeDtypeStruct((rows, out_cols), bf16),
        in_specs=[hbm] * 5,
        out_specs=vmem,
        scratch_shapes=[
            pltpu.VMEM(w_gate_up.shape, bf16),
            pltpu.VMEM(w_down.shape, bf16),
            pltpu.VMEM(expert_ids.shape[::-1], expert_ids.dtype),
            pltpu.VMEM(route_weights.shape[::-1], f32),
            pltpu.VMEM((n_e, rows, feature_cols), bf16),
            pltpu.VMEM((n_e, 8, rows), f32),
            pltpu.VMEM((n_e, 8, rows), f32),
            *[pltpu.VMEM((n_e, rows, wide), bf16)] * 6,
            *[pltpu.VMEM((n_e, rows, wide), f32)] * 2,
            pltpu.VMEM((n_e, local, rows, hidden_units), bf16),
            pltpu.VMEM((n_e, rows, out_cols), bf16),
            pltpu.VMEM((n_e, rows, out_cols), bf16),
            pltpu.VMEM((rows, out_cols), f32),
            dma((3,)),
            *[dma((local,))] * 2,
            *[dma((n_e,))] * 4,
            *[dma((parts,))] * 6,
            *[dma((parts, local))] * 2,
            *[dma((parts,))] * 2,
        ],
        compiler_params=pltpu.CompilerParams(
            collective_id=0, has_side_effects=True, vmem_limit_bytes=60 * 1024 * 1024
        ),
    )(tokens, expert_ids.T, route_weights.T, w_gate_up, w_down)


def per_device(tokens, expert_ids, route_weights, w_gate_up, w_down):
    tok_dev = tokens.shape[0]
    top_k = expert_ids.shape[1]
    local_experts = w_gate_up.shape[0]
    n_expert, n_token = lax.axis_size("expert"), lax.axis_size("token")
    experts = local_experts * n_expert
    capacity = max(2, min(tok_dev, tok_dev * top_k * 5 // (2 * experts)))
    dense = capacity >= tok_dev >= 32 and n_expert >= 2 and n_expert & (n_expert - 1) == 0
    if dense and tok_dev % 16 == 0 and n_token == local_experts == 4:
        return dense_device(tokens, expert_ids, route_weights, w_gate_up, w_down)
    return slot_device(tokens, expert_ids, route_weights, w_gate_up, w_down)


def solution(mesh):
    return jax.shard_map(
        per_device,
        mesh=mesh,
        in_specs=(
            P(("groups", "expert"), "token"),
            P(("groups", "expert"), None),
            P(("groups", "expert"), None),
            P("expert", "token", None),
            P("expert", None, "token"),
        ),
        out_specs=P(("groups", "expert"), "token"),
        check_vma=False,
    )
```

```python
import functools

import jax
import jax.numpy as jnp
from jax import lax
from jax.experimental import pallas as pl
from jax.experimental.pallas import tpu as pltpu
from jax.sharding import PartitionSpec as P

MESH = pl.DeviceIdType.MESH


def rank_slots(flat_ids, experts):
    onehot = (flat_ids[:, None] == jnp.arange(experts, dtype=jnp.int32)[None, :]).astype(jnp.int32)
    rank_of = jnp.sum((jnp.cumsum(onehot, axis=0) - 1) * onehot, axis=1)
    return (onehot, rank_of)


def gate_up_terms(inputs, w_gate_up):
    return jnp.einsum("erd,edf->ref", inputs, w_gate_up, preferred_element_type=jnp.float32)


def expert_block(inputs, gate_up_w, down_w):
    hidden_units = gate_up_w.shape[2] // 2
    summed = lax.psum_scatter(
        gate_up_terms(inputs, gate_up_w).astype(jnp.bfloat16),
        "token",
        scatter_dimension=0,
        tiled=True,
    ).astype(jnp.float32)
    hidden = (jax.nn.silu(summed[..., :hidden_units]) * summed[..., hidden_units:]).astype(
        jnp.bfloat16
    )
    produced = jnp.einsum(
        "reh,ehd->erd",
        lax.all_gather(hidden, "token", axis=0, tiled=True),
        down_w,
        preferred_element_type=jnp.float32,
    )
    return produced.astype(jnp.bfloat16)


def slot_device(tokens, expert_ids, route_weights, w_gate_up, w_down):
    tok_dev, feature_cols = tokens.shape
    top_k = expert_ids.shape[1]
    local_experts = w_gate_up.shape[0]
    n_expert = lax.axis_size("expert")
    experts = local_experts * n_expert
    capacity = max(2, min(tok_dev, tok_dev * top_k * 5 // (2 * experts)))
    slot_count = n_expert * capacity
    flat_ids = expert_ids.reshape(-1)
    onehot, rank_of = rank_slots(flat_ids, experts)
    position = (
        flat_ids % local_experts * slot_count + flat_ids // local_experts * capacity + rank_of
    )
    token_of = jnp.arange(flat_ids.shape[0], dtype=jnp.int32) // top_k
    slot_table = (
        jnp.full((local_experts * slot_count,), tok_dev, jnp.int32).at[position].set(token_of)
    )
    padded = jnp.concatenate([tokens, jnp.zeros((1, feature_cols), tokens.dtype)], axis=0)
    outgoing = jnp.take(padded, slot_table, axis=0).reshape(
        local_experts, n_expert, capacity, feature_cols
    )
    arrived = lax.all_to_all(outgoing, "expert", split_axis=1, concat_axis=1, tiled=True)
    inputs = arrived.reshape(local_experts, slot_count, feature_cols)
    expert_out = expert_block(inputs, w_gate_up, w_down)
    returned = lax.all_to_all(
        expert_out.reshape(local_experts, n_expert, capacity, feature_cols),
        "expert",
        split_axis=1,
        concat_axis=1,
        tiled=True,
    )
    picked = jnp.take(
        returned.reshape(local_experts * slot_count, feature_cols), position, axis=0
    ).reshape(tok_dev, top_k, feature_cols)
    combined = jnp.sum(route_weights[:, :, None] * picked.astype(jnp.float32), axis=1)
    return combined.astype(jnp.bfloat16)


def flip(index, bits):
    out, bit = index, 1
    while bit <= bits:
        if bits & bit:
            out = out + bit * (1 - 2 * ((index // bit) % 2))
        bit *= 2
    return out


def dense_kernel(
    chunks,
    tokens_ref,
    ids_hbm,
    weights_hbm,
    wg_hbm,
    wd_hbm,
    out_ref,
    wg,
    wd,
    ids_ref,
    weights_ref,
    tok,
    row_out,
    row_in,
    far_out,
    far_in,
    sum_out,
    sum_in,
    near_out,
    near_in,
    part,
    own,
    hid,
    back_out,
    back_in,
    total,
    load_sem,
    wg_sem,
    wd_sem,
    tok_s,
    tok_r,
    row_s,
    row_r,
    far_s,
    far_r,
    sum_s,
    sum_r,
    near_s,
    near_r,
    hid_s,
    hid_r,
    back_s,
    back_r,
):
    z = lax.axis_index("expert")
    t = lax.axis_index("token")
    rows = tokens_ref.shape[0]
    half = own.shape[2] // 2
    local = wg.shape[0]
    f32, bf16 = jnp.float32, jnp.bfloat16
    mate, across = {"token": flip(t, 1)}, {"token": flip(t, 2)}
    others = []
    for k, _, _ in chunks:
        if k and k not in others:
            others.append(k)

    barrier = pltpu.get_barrier_semaphore()
    partners = [mate, across] + [{"expert": flip(z, k)} for k in others]
    for partner in reversed(partners):
        pl.semaphore_signal(barrier, inc=1, device_id=partner, device_id_type=MESH)

    loads = [
        pltpu.make_async_copy(tokens_ref, tok.at[0], load_sem.at[0]),
        pltpu.make_async_copy(ids_hbm, ids_ref, load_sem.at[1]),
        pltpu.make_async_copy(weights_hbm, weights_ref, load_sem.at[2]),
    ]
    wg_copies, wd_copies = {}, {}
    for j in (3, 2, 1, 0):
        wg_copies[j] = pltpu.make_async_copy(wg_hbm.at[flip(t, j)], wg.at[j], wg_sem.at[j])
    for load in loads:
        load.start()
    for j in (3, 2):
        wg_copies[j].start()
    for load in loads:
        load.wait()

    for k in [0] + others:
        expert = flip(z, k) * local + t
        row = jnp.sum(
            jnp.where(ids_ref[...] == expert, weights_ref[...], 0.0), axis=0, keepdims=True
        )
        row_out[k] = jnp.broadcast_to(row, row_out.shape[1:])

    pending = []

    def send(src, dst, s_sem, r_sem, device):
        copy = pltpu.make_async_remote_copy(
            src_ref=src,
            dst_ref=dst,
            send_sem=s_sem,
            recv_sem=r_sem,
            device_id=device,
            device_id_type=MESH,
        )
        copy.start()
        pending.append(copy)
        return copy

    tok_c, row_c, far_c, sum_c, near_c, back_c = {}, {}, {}, {}, {}, {}
    hid_c = {}

    def terms(c, j):
        k, start, size = chunks[c]
        return jnp.dot(tok[k, pl.ds(start, size), :], wg[j], preferred_element_type=f32)

    def piece(c):
        k, start, size = chunks[c]
        return (k, pl.ds(start, size))

    def stage_a(c):
        k = chunks[c][0]
        here = piece(c)
        if k and chunks[c][1] == 0:
            tok_c[k].wait_recv()
        if c == 0:
            wg_copies[3].wait()
        far_out[here] = terms(c, 3).astype(bf16)
        if c == 0:
            pl.semaphore_wait(barrier, len(partners))
            for o in others:
                there = {"expert": flip(z, o)}
                tok_c[o] = send(tokens_ref, tok.at[o], tok_s.at[o], tok_r.at[o], there)
            for j in (1, 0):
                wg_copies[j].start()
        far_c[c] = send(far_out.at[here], far_in.at[here], far_s.at[c], far_r.at[c], mate)
        if c == 0:
            for j in range(local):
                wd_copies[j] = pltpu.make_async_copy(
                    wd_hbm.at[flip(t, j)], wd.at[j], wd_sem.at[j]
                )
                wd_copies[j].start()
            wg_copies[2].wait()
        part[here] = terms(c, 2)
        if c == 0:
            far_c[c].wait_recv()
            sum_out[here] = (part[here] + far_in[here].astype(f32)).astype(bf16)
            sum_c[c] = send(sum_out.at[here], sum_in.at[here], sum_s.at[c], sum_r.at[c], across)
            for o in others:
                there = {"expert": flip(z, o)}
                row_c[o] = send(row_out.at[o], row_in.at[o], row_s.at[o], row_r.at[o], there)
            wg_copies[1].wait()
        near_out[here] = terms(c, 1).astype(bf16)
        near_c[c] = send(near_out.at[here], near_in.at[here], near_s.at[c], near_r.at[c], mate)
        if c == 0:
            wg_copies[0].wait()
            own[here] = terms(c, 0)
            return
        far_c[c].wait_recv()
        sum_out[here] = (part[here] + far_in[here].astype(f32)).astype(bf16)
        sum_c[c] = send(sum_out.at[here], sum_in.at[here], sum_s.at[c], sum_r.at[c], across)
        own[here] = terms(c, 0)

    def stage_b(c):
        k, start, size = chunks[c]
        here = piece(c)
        near_c[c].wait_recv()
        if k and start == 0:
            row_c[k].wait_recv()
        row = row_in[k, :1, :] if k else row_out[k, :1, :]
        eye = start + lax.broadcasted_iota(
            jnp.int32, (size, rows), 0
        ) == lax.broadcasted_iota(jnp.int32, (size, rows), 1)
        column = jnp.sum(jnp.where(eye, row, 0.0), axis=1, keepdims=True)
        sum_c[c].wait_recv()
        gate_up = own[here] + near_in[here].astype(f32) + sum_in[here].astype(f32)
        gate, up = gate_up[:, :half], gate_up[:, half:]
        at = pl.ds(start, size)
        hid[k, 0, at] = (gate / (1.0 + jnp.exp(-gate)) * up * column).astype(bf16)
        for j, device in ((2, across), (1, mate)):
            hid_c[c, j] = send(
                hid.at[k, 0, at], hid.at[k, j, at], hid_s.at[c, j], hid_r.at[c, j], device
            )

    def stage_f(c):
        k, start, size = chunks[c]
        at = pl.ds(start, size)
        hid_c[c, 2].wait_recv()
        hid_c[c, 3] = send(
            hid.at[k, 2, at], hid.at[k, 3, at], hid_s.at[c, 3], hid_r.at[c, 3], mate
        )

    def stage_c(c):
        k, start, size = chunks[c]
        at = pl.ds(start, size)
        if c == 0:
            for j in range(local):
                wd_copies[j].wait()
        acc = jnp.dot(hid[k, 0, at], wd[0], preferred_element_type=f32)
        hid_c[c, 1].wait_recv()
        acc = acc + jnp.dot(hid[k, 1, at], wd[1], preferred_element_type=f32)
        acc = acc + jnp.dot(hid[k, 2, at], wd[2], preferred_element_type=f32)
        hid_c[c, 3].wait_recv()
        acc = acc + jnp.dot(hid[k, 3, at], wd[3], preferred_element_type=f32)
        if k:
            there = {"expert": flip(z, k)}
            back_out[k, at] = acc.astype(bf16)
            back_c[c] = send(
                back_out.at[k, at], back_in.at[k, at], back_s.at[c], back_r.at[c], there
            )
        else:
            total[at] = acc

    n = len(chunks)
    far, near = list(range(2, n - 1)), [1, n - 1]
    for step in range(n):
        stage_a(step)
        if step == 2:
            stage_b(0)
    for c in far[:1]:
        stage_b(c)
    stage_f(0)
    stage_c(0)
    for c in far[1:] + near:
        stage_b(c)
    for c in far + near:
        stage_f(c)
        stage_c(c)

    for copy in back_c.values():
        copy.wait_recv()
    result = total[...]
    for k in others:
        result = result + back_in[k].astype(f32)
    out_ref[...] = result.astype(out_ref.dtype)
    for copy in pending:
        copy.wait_send()


def dense_device(tokens, expert_ids, route_weights, w_gate_up, w_down):
    rows, feature_cols = tokens.shape
    local, _, wide = w_gate_up.shape
    hidden_units, out_cols = w_down.shape[1:]
    n_e = lax.axis_size("expert")
    first = rows // 32 * 16
    chunks = ((0, 0, rows), (1, 0, first)) + tuple((k, 0, rows) for k in range(n_e - 1, 1, -1))
    chunks += ((1, first, rows - first),)
    parts = len(chunks)
    f32, bf16 = jnp.float32, jnp.bfloat16
    vmem = pl.BlockSpec(memory_space=pltpu.VMEM)
    hbm = pl.BlockSpec(memory_space=pltpu.MemorySpace.HBM)
    dma = pltpu.SemaphoreType.DMA
    return pl.pallas_call(
        functools.partial(dense_kernel, chunks),
        out_shape=jax.ShapeDtypeStruct((rows, out_cols), bf16),
        in_specs=[hbm] * 5,
        out_specs=vmem,
        scratch_shapes=[
            pltpu.VMEM(w_gate_up.shape, bf16),
            pltpu.VMEM(w_down.shape, bf16),
            pltpu.VMEM(expert_ids.shape[::-1], expert_ids.dtype),
            pltpu.VMEM(route_weights.shape[::-1], f32),
            pltpu.VMEM((n_e, rows, feature_cols), bf16),
            pltpu.VMEM((n_e, 8, rows), f32),
            pltpu.VMEM((n_e, 8, rows), f32),
            *[pltpu.VMEM((n_e, rows, wide), bf16)] * 6,
            *[pltpu.VMEM((n_e, rows, wide), f32)] * 2,
            pltpu.VMEM((n_e, local, rows, hidden_units), bf16),
            pltpu.VMEM((n_e, rows, out_cols), bf16),
            pltpu.VMEM((n_e, rows, out_cols), bf16),
            pltpu.VMEM((rows, out_cols), f32),
            dma((3,)),
            *[dma((local,))] * 2,
            *[dma((n_e,))] * 4,
            *[dma((parts,))] * 6,
            *[dma((parts, local))] * 2,
            *[dma((parts,))] * 2,
        ],
        compiler_params=pltpu.CompilerParams(
            collective_id=0, has_side_effects=True, vmem_limit_bytes=60 * 1024 * 1024
        ),
    )(tokens, expert_ids.T, route_weights.T, w_gate_up, w_down)


def per_device(tokens, expert_ids, route_weights, w_gate_up, w_down):
    tok_dev = tokens.shape[0]
    top_k = expert_ids.shape[1]
    local_experts = w_gate_up.shape[0]
    n_expert, n_token = lax.axis_size("expert"), lax.axis_size("token")
    experts = local_experts * n_expert
    capacity = max(2, min(tok_dev, tok_dev * top_k * 5 // (2 * experts)))
    dense = capacity >= tok_dev >= 32 and n_expert >= 2 and n_expert & (n_expert - 1) == 0
    if dense and tok_dev % 16 == 0 and n_token == local_experts == 4:
        return dense_device(tokens, expert_ids, route_weights, w_gate_up, w_down)
    return slot_device(tokens, expert_ids, route_weights, w_gate_up, w_down)


def solution(mesh):
    return jax.shard_map(
        per_device,
        mesh=mesh,
        in_specs=(
            P(("groups", "expert"), "token"),
            P(("groups", "expert"), None),
            P(("groups", "expert"), None),
            P("expert", "token", None),
            P("expert", None, "token"),
        ),
        out_specs=P(("groups", "expert"), "token"),
        check_vma=False,
    )
```

```python
import functools

import jax
import jax.numpy as jnp
from jax import lax
from jax.experimental import pallas as pl
from jax.experimental.pallas import tpu as pltpu
from jax.sharding import PartitionSpec as P

MESH = pl.DeviceIdType.MESH


def rank_slots(flat_ids, experts):
    onehot = (flat_ids[:, None] == jnp.arange(experts, dtype=jnp.int32)[None, :]).astype(jnp.int32)
    rank_of = jnp.sum((jnp.cumsum(onehot, axis=0) - 1) * onehot, axis=1)
    return (onehot, rank_of)


def gate_up_terms(inputs, w_gate_up):
    return jnp.einsum("erd,edf->ref", inputs, w_gate_up, preferred_element_type=jnp.float32)


def expert_block(inputs, gate_up_w, down_w):
    hidden_units = gate_up_w.shape[2] // 2
    summed = lax.psum_scatter(
        gate_up_terms(inputs, gate_up_w).astype(jnp.bfloat16),
        "token",
        scatter_dimension=0,
        tiled=True,
    ).astype(jnp.float32)
    hidden = (jax.nn.silu(summed[..., :hidden_units]) * summed[..., hidden_units:]).astype(
        jnp.bfloat16
    )
    produced = jnp.einsum(
        "reh,ehd->erd",
        lax.all_gather(hidden, "token", axis=0, tiled=True),
        down_w,
        preferred_element_type=jnp.float32,
    )
    return produced.astype(jnp.bfloat16)


def slot_device(tokens, expert_ids, route_weights, w_gate_up, w_down):
    tok_dev, feature_cols = tokens.shape
    top_k = expert_ids.shape[1]
    local_experts = w_gate_up.shape[0]
    n_expert = lax.axis_size("expert")
    experts = local_experts * n_expert
    capacity = max(2, min(tok_dev, tok_dev * top_k * 5 // (2 * experts)))
    slot_count = n_expert * capacity
    flat_ids = expert_ids.reshape(-1)
    onehot, rank_of = rank_slots(flat_ids, experts)
    position = (
        flat_ids % local_experts * slot_count + flat_ids // local_experts * capacity + rank_of
    )
    token_of = jnp.arange(flat_ids.shape[0], dtype=jnp.int32) // top_k
    slot_table = (
        jnp.full((local_experts * slot_count,), tok_dev, jnp.int32).at[position].set(token_of)
    )
    padded = jnp.concatenate([tokens, jnp.zeros((1, feature_cols), tokens.dtype)], axis=0)
    outgoing = jnp.take(padded, slot_table, axis=0).reshape(
        local_experts, n_expert, capacity, feature_cols
    )
    arrived = lax.all_to_all(outgoing, "expert", split_axis=1, concat_axis=1, tiled=True)
    inputs = arrived.reshape(local_experts, slot_count, feature_cols)
    expert_out = expert_block(inputs, w_gate_up, w_down)
    returned = lax.all_to_all(
        expert_out.reshape(local_experts, n_expert, capacity, feature_cols),
        "expert",
        split_axis=1,
        concat_axis=1,
        tiled=True,
    )
    picked = jnp.take(
        returned.reshape(local_experts * slot_count, feature_cols), position, axis=0
    ).reshape(tok_dev, top_k, feature_cols)
    combined = jnp.sum(route_weights[:, :, None] * picked.astype(jnp.float32), axis=1)
    return combined.astype(jnp.bfloat16)


def flip(index, bits):
    out, bit = index, 1
    while bit <= bits:
        if bits & bit:
            out = out + bit * (1 - 2 * ((index // bit) % 2))
        bit *= 2
    return out


def dense_kernel(
    chunks,
    tokens_ref,
    ids_hbm,
    weights_hbm,
    wg_hbm,
    wd_hbm,
    out_ref,
    wg,
    wd,
    ids_ref,
    weights_ref,
    tok,
    row_out,
    row_in,
    far_out,
    far_in,
    sum_out,
    sum_in,
    near_out,
    near_in,
    part,
    own,
    hid,
    back_out,
    back_in,
    total,
    load_sem,
    wg_sem,
    wd_sem,
    tok_s,
    tok_r,
    row_s,
    row_r,
    far_s,
    far_r,
    sum_s,
    sum_r,
    near_s,
    near_r,
    hid_s,
    hid_r,
    back_s,
    back_r,
):
    z = lax.axis_index("expert")
    t = lax.axis_index("token")
    rows = tokens_ref.shape[0]
    half = own.shape[2] // 2
    local = wg.shape[0]
    f32, bf16 = jnp.float32, jnp.bfloat16
    mate, across = {"token": flip(t, 1)}, {"token": flip(t, 2)}
    others = []
    for k, _, _ in chunks:
        if k and k not in others:
            others.append(k)

    barrier = pltpu.get_barrier_semaphore()
    partners = [mate, across] + [{"expert": flip(z, k)} for k in others]
    for partner in reversed(partners):
        pl.semaphore_signal(barrier, inc=1, device_id=partner, device_id_type=MESH)

    loads = [
        pltpu.make_async_copy(tokens_ref, tok.at[0], load_sem.at[0]),
        pltpu.make_async_copy(ids_hbm, ids_ref, load_sem.at[1]),
        pltpu.make_async_copy(weights_hbm, weights_ref, load_sem.at[2]),
    ]
    wg_copies, wd_copies = {}, {}
    for j in (3, 2, 1, 0):
        wg_copies[j] = pltpu.make_async_copy(wg_hbm.at[flip(t, j)], wg.at[j], wg_sem.at[j])
    for load in loads:
        load.start()
    for j in (3, 2):
        wg_copies[j].start()
    for load in loads:
        load.wait()

    for k in [0] + others:
        expert = flip(z, k) * local + t
        row = jnp.sum(
            jnp.where(ids_ref[...] == expert, weights_ref[...], 0.0), axis=0, keepdims=True
        )
        row_out[k] = jnp.broadcast_to(row, row_out.shape[1:])

    pending = []

    def send(src, dst, s_sem, r_sem, device):
        copy = pltpu.make_async_remote_copy(
            src_ref=src,
            dst_ref=dst,
            send_sem=s_sem,
            recv_sem=r_sem,
            device_id=device,
            device_id_type=MESH,
        )
        copy.start()
        pending.append(copy)
        return copy

    tok_c, row_c, far_c, sum_c, near_c, back_c = {}, {}, {}, {}, {}, {}
    hid_c = {}

    def terms(c, j):
        k, start, size = chunks[c]
        return jnp.dot(tok[k, pl.ds(start, size), :], wg[j], preferred_element_type=f32)

    def piece(c):
        k, start, size = chunks[c]
        return (k, pl.ds(start, size))

    def stage_a(c):
        k = chunks[c][0]
        here = piece(c)
        if k and chunks[c][1] == 0:
            tok_c[k].wait_recv()
        if c == 0:
            pl.semaphore_wait(barrier, len(partners))
            for o in others:
                there = {"expert": flip(z, o)}
                tok_c[o] = send(tokens_ref, tok.at[o], tok_s.at[o], tok_r.at[o], there)
            for j in (1, 0):
                wg_copies[j].start()
            wg_copies[3].wait()
        far_out[here] = terms(c, 3).astype(bf16)
        far_c[c] = send(far_out.at[here], far_in.at[here], far_s.at[c], far_r.at[c], mate)
        if c == 0:
            for j in range(local):
                wd_copies[j] = pltpu.make_async_copy(
                    wd_hbm.at[flip(t, j)], wd.at[j], wd_sem.at[j]
                )
                wd_copies[j].start()
            wg_copies[2].wait()
        part[here] = terms(c, 2)
        if c == 0:
            far_c[c].wait_recv()
            sum_out[here] = (part[here] + far_in[here].astype(f32)).astype(bf16)
            sum_c[c] = send(sum_out.at[here], sum_in.at[here], sum_s.at[c], sum_r.at[c], across)
            for o in others:
                there = {"expert": flip(z, o)}
                row_c[o] = send(row_out.at[o], row_in.at[o], row_s.at[o], row_r.at[o], there)
            wg_copies[1].wait()
        near_out[here] = terms(c, 1).astype(bf16)
        near_c[c] = send(near_out.at[here], near_in.at[here], near_s.at[c], near_r.at[c], mate)
        if c == 0:
            wg_copies[0].wait()
            own[here] = terms(c, 0)
            return
        far_c[c].wait_recv()
        sum_out[here] = (part[here] + far_in[here].astype(f32)).astype(bf16)
        sum_c[c] = send(sum_out.at[here], sum_in.at[here], sum_s.at[c], sum_r.at[c], across)
        own[here] = terms(c, 0)

    def stage_b(c):
        k, start, size = chunks[c]
        here = piece(c)
        near_c[c].wait_recv()
        if k and start == 0:
            row_c[k].wait_recv()
        row = row_in[k, :1, :] if k else row_out[k, :1, :]
        eye = start + lax.broadcasted_iota(
            jnp.int32, (size, rows), 0
        ) == lax.broadcasted_iota(jnp.int32, (size, rows), 1)
        column = jnp.sum(jnp.where(eye, row, 0.0), axis=1, keepdims=True)
        sum_c[c].wait_recv()
        gate_up = own[here] + near_in[here].astype(f32) + sum_in[here].astype(f32)
        gate, up = gate_up[:, :half], gate_up[:, half:]
        at = pl.ds(start, size)
        hid[k, 0, at] = (gate / (1.0 + jnp.exp(-gate)) * up * column).astype(bf16)
        for j, device in ((2, across), (1, mate)):
            hid_c[c, j] = send(
                hid.at[k, 0, at], hid.at[k, j, at], hid_s.at[c, j], hid_r.at[c, j], device
            )

    def stage_f(c):
        k, start, size = chunks[c]
        at = pl.ds(start, size)
        hid_c[c, 2].wait_recv()
        hid_c[c, 3] = send(
            hid.at[k, 2, at], hid.at[k, 3, at], hid_s.at[c, 3], hid_r.at[c, 3], mate
        )

    def stage_c(c):
        k, start, size = chunks[c]
        at = pl.ds(start, size)
        if c == 0:
            for j in range(local):
                wd_copies[j].wait()
        acc = jnp.dot(hid[k, 0, at], wd[0], preferred_element_type=f32)
        hid_c[c, 1].wait_recv()
        acc = acc + jnp.dot(hid[k, 1, at], wd[1], preferred_element_type=f32)
        acc = acc + jnp.dot(hid[k, 2, at], wd[2], preferred_element_type=f32)
        hid_c[c, 3].wait_recv()
        acc = acc + jnp.dot(hid[k, 3, at], wd[3], preferred_element_type=f32)
        if k:
            there = {"expert": flip(z, k)}
            back_out[k, at] = acc.astype(bf16)
            back_c[c] = send(
                back_out.at[k, at], back_in.at[k, at], back_s.at[c], back_r.at[c], there
            )
        else:
            total[at] = acc

    n = len(chunks)
    far, near = list(range(2, n - 1)), [1, n - 1]
    for step in range(n):
        stage_a(step)
        if step == 2:
            stage_b(0)
    for c in far[:1]:
        stage_b(c)
    stage_f(0)
    stage_c(0)
    for c in far[1:] + near:
        stage_b(c)
    for c in far + near:
        stage_f(c)
        stage_c(c)

    for copy in back_c.values():
        copy.wait_recv()
    result = total[...]
    for k in others:
        result = result + back_in[k].astype(f32)
    out_ref[...] = result.astype(out_ref.dtype)
    for copy in pending:
        copy.wait_send()


def dense_device(tokens, expert_ids, route_weights, w_gate_up, w_down):
    rows, feature_cols = tokens.shape
    local, _, wide = w_gate_up.shape
    hidden_units, out_cols = w_down.shape[1:]
    n_e = lax.axis_size("expert")
    first = rows // 32 * 16
    chunks = ((0, 0, rows), (1, 0, first)) + tuple((k, 0, rows) for k in range(n_e - 1, 1, -1))
    chunks += ((1, first, rows - first),)
    parts = len(chunks)
    f32, bf16 = jnp.float32, jnp.bfloat16
    vmem = pl.BlockSpec(memory_space=pltpu.VMEM)
    hbm = pl.BlockSpec(memory_space=pltpu.MemorySpace.HBM)
    dma = pltpu.SemaphoreType.DMA
    return pl.pallas_call(
        functools.partial(dense_kernel, chunks),
        out_shape=jax.ShapeDtypeStruct((rows, out_cols), bf16),
        in_specs=[hbm] * 5,
        out_specs=vmem,
        scratch_shapes=[
            pltpu.VMEM(w_gate_up.shape, bf16),
            pltpu.VMEM(w_down.shape, bf16),
            pltpu.VMEM(expert_ids.shape[::-1], expert_ids.dtype),
            pltpu.VMEM(route_weights.shape[::-1], f32),
            pltpu.VMEM((n_e, rows, feature_cols), bf16),
            pltpu.VMEM((n_e, 8, rows), f32),
            pltpu.VMEM((n_e, 8, rows), f32),
            *[pltpu.VMEM((n_e, rows, wide), bf16)] * 6,
            *[pltpu.VMEM((n_e, rows, wide), f32)] * 2,
            pltpu.VMEM((n_e, local, rows, hidden_units), bf16),
            pltpu.VMEM((n_e, rows, out_cols), bf16),
            pltpu.VMEM((n_e, rows, out_cols), bf16),
            pltpu.VMEM((rows, out_cols), f32),
            dma((3,)),
            *[dma((local,))] * 2,
            *[dma((n_e,))] * 4,
            *[dma((parts,))] * 6,
            *[dma((parts, local))] * 2,
            *[dma((parts,))] * 2,
        ],
        compiler_params=pltpu.CompilerParams(
            collective_id=0, has_side_effects=True, vmem_limit_bytes=60 * 1024 * 1024
        ),
    )(tokens, expert_ids.T, route_weights.T, w_gate_up, w_down)


def per_device(tokens, expert_ids, route_weights, w_gate_up, w_down):
    tok_dev = tokens.shape[0]
    top_k = expert_ids.shape[1]
    local_experts = w_gate_up.shape[0]
    n_expert, n_token = lax.axis_size("expert"), lax.axis_size("token")
    experts = local_experts * n_expert
    capacity = max(2, min(tok_dev, tok_dev * top_k * 5 // (2 * experts)))
    dense = capacity >= tok_dev >= 32 and n_expert >= 2 and n_expert & (n_expert - 1) == 0
    if dense and tok_dev % 16 == 0 and n_token == local_experts == 4:
        return dense_device(tokens, expert_ids, route_weights, w_gate_up, w_down)
    return slot_device(tokens, expert_ids, route_weights, w_gate_up, w_down)


def solution(mesh):
    return jax.shard_map(
        per_device,
        mesh=mesh,
        in_specs=(
            P(("groups", "expert"), "token"),
            P(("groups", "expert"), None),
            P(("groups", "expert"), None),
            P("expert", "token", None),
            P("expert", None, "token"),
        ),
        out_specs=P(("groups", "expert"), "token"),
        check_vma=False,
    )
```
